32 devices in a mesh: dp: 8 (over y, x, core), mp: 4 (over z).
Axes of the slice: x: 2, y: 2, z: 4, core: 2. Of those that a mesh axis runs over, the one named last changes fastest.
Arguments:
- tokens: bfloat16 [320, 4096], P('dp'), may hold values from -6 to 6
- attn_gain: float32 [4096], replicated, may hold values from 0.1 to 1.9
- head_gain: float32 [4096], replicated, may hold values from 0.1 to 1.9
- qkv_weight: bfloat16 [4096, 3, 4096], P('dp', None, 'mp'), may hold values from -0.09375 to 0.09375
- out_weight: bfloat16 [4096, 4096], P('mp', 'dp'), may hold values from -0.09375 to 0.09375
- head_weight: bfloat16 [4096, 1024], P('mp'), may hold values from -0.09375 to 0.09375
- key_cache: bfloat16 [320, 64, 4096], P('dp', None, 'mp'), may hold values from -400 to 400
- value_cache: bfloat16 [320, 64, 4096], P('dp', None, 'mp'), may hold values from -6 to 6
- parents: int32 [320], P('dp'), may hold values from 0 to 19
- allowed: int32 [320, 2], P('dp'), may hold values from 0 to 7, all different within a row
Outputs:
- new_stream: bfloat16 [320, 4096], P('dp')
- next_logits: float32 [320, 256], P('dp', 'mp')
The draws below stay inside these ranges and needn't reach their ends.
Inputs may be any that keep to these rules, and one draw needn't show every extreme that they name: `parents`: a beam's parent is a beam of the same query. `allowed`: the 2 block ids of a beam differ.
All inputs are finite; a program needn't handle non-finite values.
Results may differ from the reference program's by a relative error of at most 0.017.
Values may be sent and summed in bfloat16 or wider, within the bound.
No kernel may reach another device: no remote copies, remote signals or barrier semaphores. Data moves between devices by JAX's collectives and lax.ppermute only.
A program may use at most 128 MiB of HBM per device.

```python
import jax
import jax.numpy as jnp
from jax import lax

D = 4096
HEAD = 128
HEADS = 32
CACHE = 64
BEAMS = 20
VOCAB = 1024
BLOCK = 128
ALLOWED = 2
QUERIES = 16
TOKENS = 320


def draw_key_cache(key, part):
    base = jnp.clip(jax.random.normal(key, (TOKENS, CACHE, D), jnp.float32), -6.0, 6.0)
    return base.astype(jnp.bfloat16)


def set_ends(array, key, smallest, top_value):
    place = [jax.random.randint(jax.random.fold_in(key, axis), (), 0, length) for axis, length in enumerate(array.shape)]
    main_axis = array.shape.index(max(array.shape))
    next_to = place[:main_axis] + [(place[main_axis] + 1) % array.shape[main_axis]] + place[main_axis + 1:]
    return array.at[tuple(place)].set(smallest).at[tuple(next_to)].set(top_value)


def block_scale(rng, shape, pieces, low, high):
    level, own = 1.0, jax.random.fold_in(rng, 6)
    for axis_at, parts in pieces:
        draws = jnp.exp(jax.random.uniform(jax.random.fold_in(own, axis_at), (parts,), jnp.float32, low / len(pieces), high / len(pieces)))
        level = level * jnp.repeat(draws, shape[axis_at] // parts).reshape([-1 if axis == axis_at else 1 for axis in range(len(shape))])
    return level


def choose_distinct(own_key, rows, amount, top, lift):
    sequence = jax.random.permutation(jax.random.fold_in(own_key, 1), amount)
    boost = sequence
    for power in range(3):
        boost = boost * boost // amount
    boost = boost * lift // amount
    lots = jax.random.randint(jax.random.fold_in(own_key, 2), (rows, amount), 0, 4096) + boost
    sure = jax.random.permutation(jax.random.fold_in(own_key, 3), rows)[jnp.arange(amount) % rows]
    lots = jnp.where(jnp.arange(rows)[:, None] == sure[None, :], 1 << 14, lots)
    score = lots * amount + jnp.arange(amount)
    return lax.top_k(score.astype(jnp.int32), top)[1].astype(jnp.int32)


def bell_draw(own_key, dims, spread, bound, pieces=(), kind=jnp.bfloat16):
    array = spread * jax.random.normal(own_key, dims, jnp.float32)
    if pieces:
        array = array * block_scale(own_key, dims, pieces, -0.22, 0.18)
    return jnp.clip(array, -bound, bound).astype(kind)


def setup_inputs(seed: int = 0) -> dict:
    seeds = jax.random.split(jax.random.key(seed), 11)
    return {
        "tokens": bell_draw(seeds[0], (TOKENS, D), 1.0, 6.0, ((0, 8),)),
        "attn_gain": jnp.clip(1.0 + 0.18 * jax.random.normal(seeds[1], (D,), jnp.float32), 0.1, 1.9),
        "head_gain": jnp.clip(1.0 + 0.18 * jax.random.normal(seeds[2], (D,), jnp.float32), 0.1, 1.9),
        "qkv_weight": bell_draw(seeds[3], (D, 3, D), D ** -0.5, 0.09375, ((0, 8), (2, 4))),
        "out_weight": bell_draw(seeds[4], (D, D), D ** -0.5, 0.09375, ((0, 4), (1, 8))),
        "head_weight": bell_draw(seeds[5], (D, VOCAB), D ** -0.5, 0.09375, ((0, 4),)),
        "key_cache": draw_key_cache(jax.random.fold_in(seeds[10], 71), 0),
        "value_cache": bell_draw(seeds[7], (TOKENS, CACHE, D), 1.0, 6.0, ((0, 8), (2, 4))),
        "parents": set_ends(jax.random.randint(seeds[8], (TOKENS,), 0, BEAMS), jax.random.fold_in(seeds[8], 1), 0, BEAMS - 1).astype(jnp.int32),
        "allowed": choose_distinct(seeds[9], TOKENS, VOCAB // BLOCK, ALLOWED, 0),
    }


def root_norm(values, gain_vec):
    float_values = values.astype(jnp.float32)
    factor = lax.rsqrt(lax.optimization_barrier(jnp.mean(float_values * float_values, axis=-1, keepdims=True)) + 1e-06)
    return float_values * factor * gain_vec

def select_blocks(whole_logits, allowed):
    block_count = whole_logits.shape[1] // BLOCK
    block_list = whole_logits.reshape(whole_logits.shape[0], block_count, BLOCK)
    one_hot_rows = (allowed[:, :, None] == jnp.arange(block_count, dtype=jnp.int32)[None, None, :]).astype(whole_logits.dtype)
    selected_token = jnp.einsum('ioh,ihp->iop', one_hot_rows, block_list, precision=lax.Precision.HIGHEST)
    return selected_token.reshape(whole_logits.shape[0], -1)

def attend(group):
    query_rows, key_new, value_new, key_old, value_previous, parent_index = group
    key_rows = jnp.concatenate([key_old[parent_index], key_new[:, None]], axis=1)
    value_rows = jnp.concatenate([value_previous[parent_index], value_new[:, None]], axis=1)
    key_rows = key_rows.reshape(BEAMS, CACHE + 1, HEADS, HEAD).astype(jnp.float32)
    value_rows = value_rows.reshape(BEAMS, CACHE + 1, HEADS, HEAD).astype(jnp.float32)
    queries = query_rows.reshape(BEAMS, HEADS, HEAD).astype(jnp.float32)
    scores = jnp.einsum('bhd,bjhd->bhj', queries, key_rows) * HEAD ** (-0.5)
    softmax_w = jax.nn.softmax(scores, axis=-1).astype(jnp.bfloat16)
    attention_result = jnp.einsum('bhj,bjhd->bhd', softmax_w.astype(jnp.float32), value_rows)
    return attention_result.astype(jnp.bfloat16).reshape(BEAMS, D)

def reference(tokens, attn_gain, head_gain, qkv_weight, out_weight, head_weight, key_cache, value_cache, parents, allowed):
    normed = root_norm(tokens, attn_gain).astype(jnp.bfloat16)
    projected = jnp.dot(normed, qkv_weight.reshape(D, 3 * D), preferred_element_type=jnp.float32)
    projected = projected.astype(jnp.bfloat16).reshape(TOKENS, 3, D)
    grouped = (projected[:, 0].reshape(QUERIES, BEAMS, D), projected[:, 1].reshape(QUERIES, BEAMS, D), projected[:, 2].reshape(QUERIES, BEAMS, D), key_cache.reshape(QUERIES, BEAMS, CACHE, D), value_cache.reshape(QUERIES, BEAMS, CACHE, D), parents.reshape(QUERIES, BEAMS))
    attention_result = lax.map(attend, grouped).reshape(TOKENS, D)
    attn_out = jnp.dot(attention_result, out_weight, preferred_element_type=jnp.float32)
    stream = tokens.astype(jnp.float32) + attn_out
    head_input = root_norm(stream, head_gain).astype(jnp.bfloat16)
    whole_logits = jnp.dot(head_input, head_weight, preferred_element_type=jnp.float32)
    return (stream.astype(jnp.bfloat16), select_blocks(whole_logits, allowed))
```

```python
import functools

import jax
import jax.numpy as jnp
from jax import lax
from jax.experimental import pallas as pl
from jax.experimental.pallas import tpu as pltpu
from jax.sharding import PartitionSpec as P

HEAD = 128
BEAMS = 20
BLOCK = 128
CORES = 2
LOW = -3e38
BF = jnp.bfloat16
F32 = jnp.float32

VM = pl.BlockSpec(memory_space=pltpu.VMEM)
SM = pl.BlockSpec(memory_space=pltpu.SMEM)


def shape(dims, kind):
    return jax.ShapeDtypeStruct(dims, kind)


def params(mib):
    return pltpu.CompilerParams(vmem_limit_bytes=mib * 2**20)


def cost(flops, moved):
    return pl.CostEstimate(flops=flops, bytes_accessed=moved, transcendentals=0)


def project_kernel(chips, place, *refs):
    pieces, (gain, own_w, other_w), outs, scratch = (
        refs[:chips],
        refs[chips : chips + 3],
        refs[chips + 3 : 2 * chips + 3],
        refs[-1],
    )
    rows = pieces[0].shape[0]
    depth = own_w.shape[1]

    @pl.when((pl.program_id(0) == 0) & (pl.program_id(1) == 0))
    def _():
        for k in range(chips):
            scratch[k * rows : (k + 1) * rows, :] = pieces[k][...].astype(F32) * gain[...]

    own_at = pl.multiple_of(place[0] * depth, depth)
    other_at = pl.multiple_of((1 - place[0]) * depth, depth)
    own_x = scratch[:, pl.ds(own_at, depth)].astype(BF)
    other_x = scratch[:, pl.ds(other_at, depth)].astype(BF)
    total = jnp.dot(own_x, own_w[0], preferred_element_type=F32) + jnp.dot(
        other_x, other_w[0], preferred_element_type=F32
    )
    for k in range(chips):
        outs[k][...] = total[k * rows : (k + 1) * rows].astype(outs[k].dtype)


def project(place, pieces, gain, own_w, other_w):
    chips = len(pieces)
    rows, width = pieces[0].shape
    _, depth, columns = own_w.shape
    tile = min(512, columns)
    steps = columns // tile
    whole = lambda dims: pl.BlockSpec(dims, lambda i, n: (0, 0))
    weight = pl.BlockSpec((1, depth, tile), lambda i, n: (i, 0, n))
    out = pl.BlockSpec((rows, tile), lambda i, n: (0, i * steps + n))
    return pl.pallas_call(
        functools.partial(project_kernel, chips),
        grid=(3, steps),
        in_specs=[SM] + [whole((rows, width))] * chips + [whole((1, width)), weight, weight],
        out_specs=[out] * chips,
        out_shape=[shape((rows, 3 * columns), BF if k else F32) for k in range(chips)],
        scratch_shapes=[pltpu.VMEM((chips * rows, width), F32)],
        compiler_params=params(24),
        cost_estimate=cost(2 * chips * rows * width * 3 * columns, 12 * depth * columns),
        name="project",
    )(place, *pieces, gain, own_w, other_w)


def attend_kernel(count, own, *refs):
    others = refs[: count - 1]
    factor, source, keys, values, out = refs[count - 1 :]
    rows, three = own.shape
    width = three // 3
    heads = width // HEAD
    cached = keys.shape[0] // rows
    total = own[...]
    for other in others:
        total += other[...].astype(F32)
    projected = (total * factor[...]).astype(BF)
    span = BEAMS * cached
    position = lax.broadcasted_iota(jnp.int32, (1, span), 1) // cached
    for group in range(rows // BEAMS):
        first = group * BEAMS
        low = first // 8 * 8
        high = -(-(first + BEAMS) // 8) * 8
        window = projected[low:high]
        parent = source[low:high] - first
        bias = jnp.where(position == parent, 0.0, LOW)
        token = lax.broadcasted_iota(jnp.int32, (high - low, 1), 0) + low
        mine = (token >= first) & (token < first + BEAMS)
        for head in range(heads):
            at = slice(head * HEAD, (head + 1) * HEAD)
            query = window[:, at]
            new_key = window[:, width + head * HEAD : width + (head + 1) * HEAD]
            new_value = window[:, 2 * width + head * HEAD : 2 * width + (head + 1) * HEAD]
            block = keys[first * cached : first * cached + span, at]
            score = (
                lax.dot_general(
                    query, block, (((1,), (1,)), ((), ())), preferred_element_type=F32
                )
                * HEAD ** (-0.5)
                + bias
            )
            new_score = jnp.sum(
                query.astype(F32) * new_key.astype(F32), axis=1, keepdims=True
            ) * HEAD ** (-0.5)
            top = jnp.maximum(jnp.max(score, axis=1, keepdims=True), new_score)
            weight = jnp.exp(score - top)
            new_weight = jnp.exp(new_score - top)
            scale = 1.0 / (jnp.sum(weight, axis=1, keepdims=True) + new_weight)
            weight = (weight * scale).astype(BF)
            new_weight = (new_weight * scale).astype(BF).astype(F32)
            result = (
                jnp.dot(
                    weight,
                    values[first * cached : first * cached + span, at],
                    preferred_element_type=F32,
                )
                + new_weight * new_value.astype(F32)
            )
            if low == first:
                out[low:high, at] = result.astype(out.dtype)
            else:
                out[low:high, at] = jnp.where(
                    mine, result, out[low:high, at].astype(F32)
                ).astype(out.dtype)


def attend(parts, factor, source, keys, values):
    rows, three = parts[0].shape
    width = three // 3
    span = keys.shape[0]
    return pl.pallas_call(
        functools.partial(attend_kernel, len(parts)),
        in_specs=[VM] * (len(parts) + 4),
        out_specs=VM,
        out_shape=shape((rows, width), BF),
        compiler_params=params(40),
        cost_estimate=cost(4 * rows * span * width, 4 * span * width),
        name="attend",
    )(*parts, factor, source, keys, values)


def output_kernel(chips, place, *refs):
    pieces, (own_w, other_w), outs = refs[:chips], refs[chips : chips + 2], refs[chips + 2 :]
    rows = pieces[0].shape[0]
    half = own_w.shape[1]
    joined = jnp.concatenate([piece[...].astype(F32) for piece in pieces], axis=0).astype(BF)
    for at, weight in ((place[0], own_w), (1 - place[0], other_w)):
        columns = pl.ds(pl.multiple_of(at * half, half), half)
        total = jnp.dot(joined, weight[...], preferred_element_type=F32)
        for k in range(chips):
            outs[k][:, columns] = total[k * rows : (k + 1) * rows].astype(BF)


def output(place, pieces, own_w, other_w):
    chips = len(pieces)
    rows = pieces[0].shape[0]
    width, half = own_w.shape
    return pl.pallas_call(
        functools.partial(output_kernel, chips),
        in_specs=[SM] + [VM] * (chips + 2),
        out_specs=[VM] * chips,
        out_shape=[shape((rows, CORES * half), BF)] * chips,
        compiler_params=params(16),
        cost_estimate=cost(4 * chips * rows * width * half, 4 * width * half),
        name="output",
    )(place, *pieces, own_w, other_w)


def logits_kernel(count, place, stream, gain, weight, allowed, *outs):
    value = stream[...]
    rows = value.shape[0]
    square = jnp.sum(value * value, axis=1, keepdims=True)
    whole = jnp.dot(
        (value * gain[...]).astype(BF), weight[...], preferred_element_type=F32
    )
    picked = []
    for slot in range(allowed.shape[1]):
        wanted = allowed[:, slot : slot + 1]
        total = jnp.zeros((rows, BLOCK), F32)
        for block in range(whole.shape[1] // BLOCK):
            total = jnp.where(
                wanted == block, whole[:, block * BLOCK : (block + 1) * BLOCK], total
            )
        picked.append(total)
    picked = jnp.concatenate(picked, axis=1)
    share = picked.shape[1] // count
    wide = outs[0].shape[1]
    lane = lax.broadcasted_iota(jnp.int32, (rows, wide), 1)
    tail = jnp.where(lane == share, square, 0.0)
    blocks = []
    for target in range(count):
        cut = picked[:, target * share : (target + 1) * share]
        blocks.append(jnp.concatenate([cut, tail[:, share:]], axis=1))
    for shift in range(count):
        target = lax.rem(place[1] + shift, count)
        total = blocks[0]
        for index in range(1, count):
            total = jnp.where(target == index, blocks[index], total)
        outs[shift][...] = total


def logits(place, stream, gain, weight, allowed, count):
    rows = stream.shape[0]
    share = allowed.shape[1] * BLOCK // count
    wide = (share + BLOCK) // BLOCK * BLOCK
    return pl.pallas_call(
        functools.partial(logits_kernel, count),
        in_specs=[SM] + [VM] * 4,
        out_specs=[VM] * count,
        out_shape=[shape((rows, wide), F32)] * count,
        compiler_params=params(16),
        cost_estimate=cost(2 * rows * weight.shape[0] * weight.shape[1], 2 * weight.size),
        name="logits",
    )(place, stream, gain, weight, allowed)


def finish_kernel(count, share, features, place, *refs):
    streams, sums, (stream_out, logits_out) = refs[:count], refs[count : 2 * count], refs[-2:]
    width = streams[0].shape[1]
    for shift in range(count):
        owner = lax.rem(place[1] + count - shift, count)
        columns = pl.ds(pl.multiple_of(owner * width, width), width)
        stream_out[:, columns] = streams[shift][...]
    total = sums[0][...]
    for shift in range(1, count):
        total += sums[shift][...]
    factor = lax.rsqrt(total[:, share : share + 1] * (1.0 / features) + 1e-06)
    logits_out[...] = total[:, :share] * factor


def finish(place, streams, sums, share):
    count = len(streams)
    rows, width = streams[0].shape
    return pl.pallas_call(
        functools.partial(finish_kernel, count, share, count * width),
        in_specs=[SM] + [VM] * (2 * count),
        out_specs=[VM, VM],
        out_shape=[shape((rows, count * width), BF), shape((rows, share), F32)],
        compiler_params=params(8),
        name="finish",
    )(place, *streams, *sums)


def on_device(
    dp,
    mp,
    tokens,
    attn_gain,
    head_gain,
    qkv_weight,
    out_weight,
    head_weight,
    key_cache,
    value_cache,
    parents,
    allowed,
):
    chips = dp // CORES
    rows, features = tokens.shape
    wide = features // chips
    here = lax.axis_index("dp")
    level = lax.axis_index("mp")
    chip, core = here // CORES, here % CORES
    place = jnp.stack([core, level]).astype(jnp.int32)

    def to_chip(value, k):
        return lax.ppermute(value, "dp", [(i, i ^ (CORES * k)) for i in range(dp)])

    def to_level(value, m):
        return lax.ppermute(value, "mp", [(i, (i + m) % mp) for i in range(mp)])

    def to_core(value):
        return lax.ppermute(value, "dp", [(i, i ^ 1) for i in range(dp)])

    def columns_of(value, index, width):
        return lax.dynamic_slice_in_dim(value, index * width, width, value.ndim - 1)

    blocks = [columns_of(tokens, chip ^ k, wide) for k in range(chips)]
    pieces = blocks[:1] + [to_chip(blocks[k], k) for k in range(1, chips)]
    own_qkv = jnp.transpose(qkv_weight, (1, 0, 2))
    other_qkv = to_core(own_qkv)
    other_out = to_core(out_weight)
    float_tokens = tokens.astype(F32)
    factor = lax.rsqrt(jnp.mean(float_tokens * float_tokens, axis=-1, keepdims=True) + 1e-06)
    gain = columns_of(attn_gain[None], chip, wide)

    parts = list(project(place, pieces, gain, own_qkv, other_qkv))
    parts = parts[:1] + [to_chip(parts[k], k) for k in range(1, chips)]

    source = jnp.arange(rows, dtype=jnp.int32) // BEAMS * BEAMS + parents
    head_width = key_cache.shape[2]
    attended = attend(
        parts,
        factor,
        source[:, None],
        key_cache.reshape(-1, head_width),
        value_cache.reshape(-1, head_width),
    )

    pieces = [attended] + [to_chip(attended, k) for k in range(1, chips)]
    parts = list(output(place, pieces, out_weight, other_out))
    parts = jnp.stack(parts[:1] + [to_chip(parts[k], k) for k in range(1, chips)])
    slices = [
        lax.dynamic_index_in_dim(parts, chip ^ ((level + m) % mp), 0, keepdims=False)
        for m in range(mp)
    ]
    total = slices[0].astype(F32)
    for m in range(1, mp):
        total += to_level(slices[m], m).astype(F32)
    stream = columns_of(tokens, level, wide).astype(F32) + total

    rounded = stream.astype(BF)
    streams = [rounded] + [to_level(rounded, m) for m in range(1, mp)]
    sums = logits(
        place, stream, columns_of(head_gain[None], level, wide), head_weight, allowed, mp
    )
    sums = list(sums[:1]) + [to_level(sums[m], m) for m in range(1, mp)]
    return tuple(finish(place, streams, sums, allowed.shape[1] * BLOCK // mp))


def solution(mesh):
    in_specs = (
        P("dp", None),
        P(),
        P(),
        P("dp", None, "mp"),
        P("mp", "dp"),
        P("mp", None),
        P("dp", None, "mp"),
        P("dp", None, "mp"),
        P("dp"),
        P("dp", None),
    )
    out_specs = (P("dp", None), P("dp", "mp"))
    return jax.shard_map(
        functools.partial(on_device, mesh.shape["dp"], mesh.shape["mp"]),
        mesh=mesh,
        in_specs=in_specs,
        out_specs=out_specs,
        check_vma=False,
    )
```

```python
import functools

import jax
import jax.numpy as jnp
from jax import lax
from jax.experimental import pallas as pl
from jax.experimental.pallas import tpu as pltpu
from jax.sharding import PartitionSpec as P

HEAD = 128
BEAMS = 20
BLOCK = 128
CORES = 2
LOW = -3e38
BF = jnp.bfloat16
F32 = jnp.float32

VM = pl.BlockSpec(memory_space=pltpu.VMEM)
SM = pl.BlockSpec(memory_space=pltpu.SMEM)
ANY = pl.BlockSpec(memory_space=pl.ANY)


def shape(dims, kind):
    return jax.ShapeDtypeStruct(dims, kind)


def params(mib):
    return pltpu.CompilerParams(vmem_limit_bytes=mib * 2**20)


def cost(flops, moved):
    return pl.CostEstimate(flops=flops, bytes_accessed=moved, transcendentals=0)


def split_kernel(chips, place, tokens, *refs):
    outs, sems = refs[: chips + 1], refs[chips + 1]
    width = outs[0].shape[1]
    copies = []
    for k in range(chips + 1):
        index = place[2] ^ k if k < chips else place[1]
        columns = pl.ds(pl.multiple_of(index * width, width), width)
        copies.append(pltpu.make_async_copy(tokens.at[:, columns], outs[k], sems.at[k]))
    for copy in copies[1:] + copies[:1]:
        copy.start()
    for copy in copies:
        copy.wait()


def split(place, tokens, chips):
    rows, features = tokens.shape
    return pl.pallas_call(
        functools.partial(split_kernel, chips),
        in_specs=[SM, ANY],
        out_specs=[VM] * (chips + 1),
        out_shape=[shape((rows, features // chips), tokens.dtype)] * (chips + 1),
        scratch_shapes=[pltpu.SemaphoreType.DMA((chips + 1,))],
        compiler_params=params(4),
        cost_estimate=cost(0, 4 * tokens.size),
        name="split",
    )(place, tokens)


def fetch_kernel(count, *refs):
    sources, targets, sems = refs[:count], refs[count : 2 * count], refs[2 * count]
    copies = []
    for i in range(count):
        pieces = 4 if sources[i].shape[0] % 32 == 0 else 1
        size = sources[i].shape[0] // pieces
        for n in range(pieces):
            part = pl.ds(n * size, size)
            copies.append(
                pltpu.make_async_copy(
                    sources[i].at[part], targets[i].at[part], sems.at[4 * i + n]
                )
            )
    for copy in copies:
        copy.start()
    for copy in copies:
        copy.wait()


def fetch(name, *sources):
    count = len(sources)
    return pl.pallas_call(
        functools.partial(fetch_kernel, count),
        in_specs=[ANY] * count,
        out_specs=[VM] * count,
        out_shape=[shape(source.shape, source.dtype) for source in sources],
        scratch_shapes=[pltpu.SemaphoreType.DMA((4 * count,))],
        compiler_params=params(16),
        cost_estimate=cost(0, sum(4 * source.size for source in sources)),
        name=name,
    )(*sources)


def project_kernel(chips, place, *refs):
    pieces, (gain, own_w, other_w) = refs[:chips], refs[chips : chips + 3]
    outs, scratch = refs[chips + 3 : 2 * chips + 3], refs[-1]
    rows, width = pieces[0].shape
    depth = own_w.shape[0] // 3
    columns = own_w.shape[1]
    scaled = gain[:, pl.ds(pl.multiple_of(place[2] * width, width), width)]
    for k in range(chips):
        scratch[k * rows : (k + 1) * rows, :] = pieces[k][...].astype(F32) * scaled
    own_at = pl.multiple_of(place[0] * depth, depth)
    other_at = pl.multiple_of((1 - place[0]) * depth, depth)
    own_x = scratch[:, pl.ds(own_at, depth)].astype(BF)
    other_x = scratch[:, pl.ds(other_at, depth)].astype(BF)
    tile = min(512, columns)
    for i in range(3):
        for n in range(columns // tile):
            at = slice(n * tile, (n + 1) * tile)
            total = jnp.dot(
                own_x, own_w[i * depth : (i + 1) * depth, at], preferred_element_type=F32
            ) + jnp.dot(
                other_x, other_w[i * depth : (i + 1) * depth, at], preferred_element_type=F32
            )
            to = slice(i * columns + n * tile, i * columns + (n + 1) * tile)
            for k in range(chips):
                outs[k][:, to] = total[k * rows : (k + 1) * rows].astype(BF)


def project(place, pieces, gain, own_w, other_w):
    chips = len(pieces)
    rows, width = pieces[0].shape
    columns = own_w.shape[1]
    return pl.pallas_call(
        functools.partial(project_kernel, chips),
        in_specs=[SM] + [VM] * (chips + 3),
        out_specs=[VM] * chips,
        out_shape=[shape((rows, 3 * columns), BF)] * chips,
        scratch_shapes=[pltpu.VMEM((chips * rows, width), F32)],
        compiler_params=params(12),
        cost_estimate=cost(2 * chips * rows * width * 3 * columns, 4 * own_w.size),
        name="project",
    )(place, *pieces, gain, own_w, other_w)


def attend_kernel(count, *refs):
    parts = refs[:count]
    tokens, source, keys, values, out, scores, sums = refs[count:]
    rows, three = parts[0].shape
    width = three // 3
    heads = width // HEAD
    cached = keys.shape[0] // rows
    total = parts[0][...].astype(F32)
    for part in parts[1:]:
        total += part[...].astype(F32)
    stream = tokens[...].astype(F32)
    factor = lax.rsqrt(jnp.mean(stream * stream, axis=1, keepdims=True) + 1e-06)
    projected = (total * factor).astype(BF)
    span = BEAMS * cached
    groups = rows // BEAMS
    position = lax.broadcasted_iota(jnp.int32, (1, span), 1) // cached
    windows = []
    for group in range(groups):
        first = group * BEAMS
        windows.append((first // 8 * 8, -(-(first + BEAMS) // 8) * 8))
    size = max(high - low for low, high in windows)
    for group, (low, high) in enumerate(windows):
        for head in range(heads):
            at = slice(head * HEAD, (head + 1) * HEAD)
            block = keys[group * span : (group + 1) * span, at]
            place = (group * heads + head) * size
            scores[place : place + high - low, :] = lax.dot_general(
                projected[low:high, at],
                block,
                (((1,), (1,)), ((), ())),
                preferred_element_type=F32,
            )
    unit = HEAD ** (-0.5) * 1.4426950408889634
    news = []
    for group, (low, high) in enumerate(windows):
        first = group * BEAMS
        bias = jnp.where(position == source[low:high] - first, 0.0, LOW)
        for head in range(heads):
            at = slice(head * HEAD, (head + 1) * HEAD)
            key_at = slice(width + head * HEAD, width + (head + 1) * HEAD)
            place = (group * heads + head) * size
            score = scores[place : place + high - low, :] * unit + bias
            new_score = (
                jnp.sum(
                    projected[low:high, at].astype(F32) * projected[low:high, key_at].astype(F32),
                    axis=1,
                    keepdims=True,
                )
                * unit
            )
            top = jnp.maximum(jnp.max(score, axis=1, keepdims=True), new_score)
            weight = jnp.exp2(score - top)
            new_weight = jnp.exp2(new_score - top)
            scale = 1.0 / (jnp.sum(weight, axis=1, keepdims=True) + new_weight)
            sums[place : place + high - low, :] = weight.astype(BF).astype(F32)
            news.append((new_weight, scale))
    for group, (low, high) in enumerate(windows):
        first = group * BEAMS
        token = lax.broadcasted_iota(jnp.int32, (high - low, 1), 0) + low
        mine = (token >= first) & (token < first + BEAMS)
        for head in range(heads):
            at = slice(head * HEAD, (head + 1) * HEAD)
            value_at = slice(2 * width + head * HEAD, 2 * width + (head + 1) * HEAD)
            place = (group * heads + head) * size
            new_weight, scale = news[group * heads + head]
            result = (
                jnp.dot(
                    sums[place : place + high - low, :].astype(BF),
                    values[group * span : (group + 1) * span, at],
                    preferred_element_type=F32,
                )
                + new_weight.astype(BF).astype(F32) * projected[low:high, value_at].astype(F32)
            ) * scale
            if low == first:
                out[low:high, at] = result.astype(out.dtype)
            else:
                out[low:high, at] = jnp.where(
                    mine, result, out[low:high, at].astype(F32)
                ).astype(out.dtype)


def attend(parts, tokens, source, keys, values):
    rows, three = parts[0].shape
    width = three // 3
    cached = keys.shape[0] // rows
    stack = rows // BEAMS * (width // HEAD) * (-(-BEAMS // 8) * 8 + 8)
    return pl.pallas_call(
        functools.partial(attend_kernel, len(parts)),
        in_specs=[VM] * (len(parts) + 4),
        out_specs=VM,
        out_shape=shape((rows, width), BF),
        scratch_shapes=[pltpu.VMEM((stack, BEAMS * cached), F32)] * 2,
        compiler_params=params(14),
        cost_estimate=cost(4 * rows * BEAMS * cached * width, 4 * keys.size),
        name="attend",
    )(*parts, tokens, source, keys, values)


def output_kernel(chips, place, *refs):
    pieces, (own_w, other_w), outs = refs[:chips], refs[chips : chips + 2], refs[chips + 2 :]
    rows = pieces[0].shape[0]
    half = own_w.shape[1]
    joined = jnp.concatenate([piece[...].astype(F32) for piece in pieces], axis=0).astype(BF)
    for at, weight in ((place[0], own_w), (1 - place[0], other_w)):
        columns = pl.ds(pl.multiple_of(at * half, half), half)
        total = jnp.dot(joined, weight[...], preferred_element_type=F32)
        for k in range(chips):
            outs[k][:, columns] = total[k * rows : (k + 1) * rows].astype(BF)


def output(place, pieces, own_w, other_w):
    chips = len(pieces)
    rows = pieces[0].shape[0]
    width, half = own_w.shape
    return pl.pallas_call(
        functools.partial(output_kernel, chips),
        in_specs=[SM] + [VM] * (chips + 2),
        out_specs=[VM] * chips,
        out_shape=[shape((rows, CORES * half), BF)] * chips,
        compiler_params=params(16),
        cost_estimate=cost(4 * chips * rows * width * half, 4 * width * half),
        name="output",
    )(place, *pieces, own_w, other_w)


def logits_kernel(count, place, *refs):
    partials, (tokens, gain, weight, allowed) = refs[:count], refs[count : count + 4]
    own_stream, own_tail, outs = refs[count + 4], refs[count + 5], refs[count + 6 :]
    rows, width = tokens.shape
    value = partials[0][...].astype(F32)
    for partial in partials[1:]:
        value += partial[...].astype(F32)
    value += tokens[...].astype(F32)
    rounded = value.astype(BF)
    own_stream[...] = rounded
    for out in outs:
        out[:, :width] = rounded
    square = jnp.sum(value * value, axis=1, keepdims=True)
    scaled = gain[:, pl.ds(pl.multiple_of(place[1] * width, width), width)]
    whole = jnp.dot((value * scaled).astype(BF), weight[...], preferred_element_type=F32)
    picked = []
    for slot in range(allowed.shape[1]):
        wanted = allowed[:, slot : slot + 1]
        total = jnp.zeros((rows, BLOCK), F32)
        for block in range(whole.shape[1] // BLOCK):
            total = jnp.where(
                wanted == block, whole[:, block * BLOCK : (block + 1) * BLOCK], total
            )
        picked.append(total)
    picked = jnp.concatenate(picked, axis=1)
    share = picked.shape[1] // count
    wide = own_tail.shape[1]
    lane = lax.broadcasted_iota(jnp.int32, (rows, wide), 1)
    coarse = square.astype(BF).astype(F32)
    tail = jnp.where(lane == share, coarse, jnp.where(lane == share + 1, square - coarse, 0.0))
    blocks = []
    for target in range(count):
        cut = picked[:, target * share : (target + 1) * share]
        blocks.append(jnp.concatenate([cut, tail[:, share:]], axis=1))
    for shift in range(count):
        target = lax.rem(place[1] + shift, count)
        total = blocks[0]
        for index in range(1, count):
            total = jnp.where(target == index, blocks[index], total)
        if shift == 0:
            own_tail[...] = total
        else:
            outs[shift - 1][:, width:] = total.astype(BF)


def logits(place, partials, tokens, gain, weight, allowed):
    count = len(partials)
    rows, width = tokens.shape
    share = allowed.shape[1] * BLOCK // count
    wide = (share + 1 + BLOCK) // BLOCK * BLOCK
    return pl.pallas_call(
        functools.partial(logits_kernel, count),
        in_specs=[SM] + [VM] * (count + 4),
        out_specs=[VM] * (count + 1),
        out_shape=[shape((rows, width), BF), shape((rows, wide), F32)]
        + [shape((rows, width + wide), BF)] * (count - 1),
        compiler_params=params(8),
        cost_estimate=cost(2 * rows * weight.shape[0] * weight.shape[1], 2 * weight.size),
        name="logits",
    )(place, *partials, tokens, gain, weight, allowed)


def finish_kernel(count, share, place, own_stream, own_tail, *refs):
    others, (stream_out, logits_out) = refs[: count - 1], refs[-2:]
    width = own_stream.shape[1]

    def columns(shift):
        owner = lax.rem(place[1] + count - shift, count)
        return pl.ds(pl.multiple_of(owner * width, width), width)

    stream_out[:, columns(0)] = own_stream[...]
    total = own_tail[...]
    for shift in range(1, count):
        stream_out[:, columns(shift)] = others[shift - 1][:, :width]
        total += others[shift - 1][:, width:].astype(F32)
    square = total[:, share : share + 1] + total[:, share + 1 : share + 2]
    factor = lax.rsqrt(square * (1.0 / (count * width)) + 1e-06)
    logits_out[...] = total[:, :share] * factor


def finish(place, own_stream, own_tail, others, share):
    count = len(others) + 1
    rows, width = own_stream.shape
    return pl.pallas_call(
        functools.partial(finish_kernel, count, share),
        in_specs=[SM] + [VM] * (count + 1),
        out_specs=[VM, VM],
        out_shape=[shape((rows, count * width), BF), shape((rows, share), F32)],
        compiler_params=params(4),
        name="finish",
    )(place, own_stream, own_tail, *others)


def on_device(
    dp,
    mp,
    tokens,
    attn_gain,
    head_gain,
    qkv_weight,
    out_weight,
    head_weight,
    key_cache,
    value_cache,
    parents,
    allowed,
):
    chips = dp // CORES
    rows = tokens.shape[0]
    here = lax.axis_index("dp")
    level = lax.axis_index("mp")
    chip, core = here // CORES, here % CORES
    place = jnp.stack([core, level, chip]).astype(jnp.int32)

    def to_chip(value, k):
        return lax.ppermute(value, "dp", [(i, i ^ (CORES * k)) for i in range(dp)])

    def to_level(value, m):
        return lax.ppermute(value, "mp", [(i, (i + m) % mp) for i in range(mp)])

    def to_core(value):
        return lax.ppermute(value, "dp", [(i, i ^ 1) for i in range(dp)])

    *blocks, level_tokens = split(place, tokens, chips)
    pieces = blocks[:1] + [to_chip(blocks[k], k) for k in range(1, chips)]
    own_qkv = jnp.transpose(qkv_weight, (1, 0, 2)).reshape(-1, qkv_weight.shape[2])
    other_qkv = to_core(own_qkv)
    other_out = to_core(out_weight)
    own_qkv, _ = lax.optimization_barrier((own_qkv, blocks[0]))
    (own_qkv,) = fetch("fetch_qkv", own_qkv)

    parts = list(project(place, pieces, attn_gain[None], own_qkv, other_qkv))
    head_width = key_cache.shape[2]
    caches = (key_cache.reshape(-1, head_width), value_cache.reshape(-1, head_width))
    caches, _ = lax.optimization_barrier((caches, parts[0]))
    keys, values = fetch("fetch_cache", *caches)
    parts = parts[:1] + [to_chip(parts[k], k) for k in range(1, chips)]

    source = jnp.arange(rows, dtype=jnp.int32) // BEAMS * BEAMS + parents
    attended = attend(parts, tokens, source[:, None], keys, values)

    pieces = [attended] + [to_chip(attended, k) for k in range(1, chips)]
    parts = list(output(place, pieces, out_weight, other_out))
    parts = jnp.stack(parts[:1] + [to_chip(parts[k], k) for k in range(1, chips)])
    slices = [
        lax.dynamic_index_in_dim(parts, chip ^ ((level + m) % mp), 0, keepdims=False)
        for m in range(mp)
    ]
    slices = slices[:1] + [to_level(slices[m], m) for m in range(1, mp)]
    own_stream, own_tail, *others = logits(
        place, slices, level_tokens, head_gain[None], head_weight, allowed
    )
    others = [to_level(other, m + 1) for m, other in enumerate(others)]
    return tuple(finish(place, own_stream, own_tail, others, allowed.shape[1] * BLOCK // mp))


def solution(mesh):
    in_specs = (
        P("dp", None),
        P(),
        P(),
        P("dp", None, "mp"),
        P("mp", "dp"),
        P("mp", None),
        P("dp", None, "mp"),
        P("dp", None, "mp"),
        P("dp"),
        P("dp", None),
    )
    out_specs = (P("dp", None), P("dp", "mp"))
    return jax.shard_map(
        functools.partial(on_device, mesh.shape["dp"], mesh.shape["mp"]),
        mesh=mesh,
        in_specs=in_specs,
        out_specs=out_specs,
        check_vma=False,
    )
```

```python
import functools

import jax
import jax.numpy as jnp
from jax import lax
from jax.experimental import pallas as pl
from jax.experimental.pallas import tpu as pltpu
from jax.sharding import PartitionSpec as P

HEAD = 128
BEAMS = 20
BLOCK = 128
CORES = 2
PIECES = 4
LOW = -3e38
LOG2E = 1.4426950408889634
BF = jnp.bfloat16
F32 = jnp.float32

VM = pl.BlockSpec(memory_space=pltpu.VMEM)
SM = pl.BlockSpec(memory_space=pltpu.SMEM)
HB = pl.BlockSpec(memory_space=pltpu.HBM)


def shape(dims, kind):
    return jax.ShapeDtypeStruct(dims, kind)


def params(mib):
    return pltpu.CompilerParams(vmem_limit_bytes=mib * 2**20)


def cost(flops, moved):
    return pl.CostEstimate(flops=flops, bytes_accessed=moved, transcendentals=0)


def split_kernel(chips, place, tokens, *refs):
    outs, sems = refs[: chips + 1], refs[chips + 1]
    width = outs[0].shape[1]
    copies = []
    for k in range(chips + 1):
        index = place[2] ^ k if k < chips else place[1]
        columns = pl.ds(pl.multiple_of(index * width, width), width)
        copies.append(pltpu.make_async_copy(tokens.at[:, columns], outs[k], sems.at[k]))
    for copy in copies[1:] + copies[:1]:
        copy.start()
    for copy in copies:
        copy.wait()


def split(place, tokens, chips):
    rows, features = tokens.shape
    return pl.pallas_call(
        functools.partial(split_kernel, chips),
        in_specs=[SM, HB],
        out_specs=[VM] * (chips + 1),
        out_shape=[shape((rows, features // chips), tokens.dtype)] * (chips + 1),
        scratch_shapes=[pltpu.SemaphoreType.DMA((chips + 1,))],
        compiler_params=params(4),
        cost_estimate=cost(0, 4 * tokens.size),
        name="split",
    )(place, in_hbm(tokens))


def fetch_kernel(count, *refs):
    sources, targets, sems = refs[:count], refs[count : 2 * count], refs[2 * count]
    copies = []
    for i in range(count):
        size = targets[i].shape[0] // PIECES
        for n in range(PIECES):
            part = pl.ds(n * size, size)
            copies.append(
                pltpu.make_async_copy(
                    sources[i].at[part], targets[i].at[part], sems.at[PIECES * i + n]
                )
            )
    for copy in copies:
        copy.start()
    for copy in copies:
        copy.wait()


def fetch(name, *sources):
    count = len(sources)
    return pl.pallas_call(
        functools.partial(fetch_kernel, count),
        in_specs=[HB] * count,
        out_specs=[VM] * count,
        out_shape=[shape(source.shape, source.dtype) for source in sources],
        scratch_shapes=[pltpu.SemaphoreType.DMA((PIECES * count,))],
        compiler_params=params(2),
        cost_estimate=cost(0, sum(4 * source.size for source in sources)),
        name=name,
    )(*[in_hbm(source) for source in sources])


def in_hbm(value):
    return pltpu.with_memory_space_constraint(value, pltpu.HBM)


def scale_pieces(place, pieces, gain, scratch):
    rows, width = pieces[0].shape
    scaled = gain[:, pl.ds(pl.multiple_of(place[2] * width, width), width)]
    for k, piece in enumerate(pieces):
        scratch[k * rows : (k + 1) * rows, :] = piece[...].astype(F32) * scaled
    half = width // CORES
    own = pl.ds(pl.multiple_of(place[0] * half, half), half)
    other = pl.ds(pl.multiple_of((1 - place[0]) * half, half), half)
    return scratch[:, own].astype(BF), scratch[:, other].astype(BF)


def multiply(own_x, other_x, own_w, other_w, kinds, outs):
    rows = outs[0].shape[0]
    depth, columns = own_w.shape[0] // 3, own_w.shape[1]
    tile = min(512, columns)
    for index, kind in enumerate(kinds):
        at = slice(kind * depth, (kind + 1) * depth)
        for n in range(columns // tile):
            to = slice(n * tile, (n + 1) * tile)
            total = jnp.dot(own_x, own_w[at, to], preferred_element_type=F32) + jnp.dot(
                other_x, other_w[at, to], preferred_element_type=F32
            )
            where = slice(index * columns + n * tile, index * columns + (n + 1) * tile)
            for k, out in enumerate(outs):
                out[:, where] = total[k * rows : (k + 1) * rows].astype(BF)


def query_kernel(chips, place, *refs):
    pieces, (gain, own_w, other_w) = refs[:chips], refs[chips : chips + 3]
    outs, (own_x, other_x, scratch) = refs[chips + 3 : 2 * chips + 3], refs[-3:]
    own, other = scale_pieces(place, pieces, gain, scratch)
    own_x[...] = own
    other_x[...] = other
    multiply(own, other, own_w, other_w, (0,), outs)


def project_query(place, pieces, gain, own_w, other_w):
    chips = len(pieces)
    rows, width = pieces[0].shape
    columns = own_w.shape[1]
    return pl.pallas_call(
        functools.partial(query_kernel, chips),
        in_specs=[SM] + [VM] * (chips + 3),
        out_specs=[VM] * (chips + 2),
        out_shape=[shape((rows, columns), BF)] * chips
        + [shape((chips * rows, width // CORES), BF)] * 2,
        scratch_shapes=[pltpu.VMEM((chips * rows, width), F32)],
        compiler_params=params(8),
        cost_estimate=cost(2 * chips * rows * width * columns, 4 * width * columns),
        name="query",
    )(place, *pieces, gain, own_w, other_w)


def pair_kernel(own_x, other_x, own_w, other_w, *outs):
    multiply(own_x[...], other_x[...], own_w, other_w, (1, 2), outs)


def project_pair(own_x, other_x, own_w, other_w, chips):
    rows = own_x.shape[0] // chips
    columns = own_w.shape[1]
    return pl.pallas_call(
        pair_kernel,
        in_specs=[VM] * 4,
        out_specs=[VM] * chips,
        out_shape=[shape((rows, 2 * columns), BF)] * chips,
        compiler_params=params(8),
        cost_estimate=cost(4 * own_x.size * 2 * columns, 8 * own_x.shape[1] * columns),
        name="pair",
    )(own_x, other_x, own_w, other_w)


def column_of(row):
    count = row.shape[1]
    at = lax.broadcasted_iota(jnp.int32, (count, count), 0)
    to = lax.broadcasted_iota(jnp.int32, (count, count), 1)
    return jnp.sum(jnp.where(at == to, row.astype(F32), 0.0), axis=1, keepdims=True).astype(
        jnp.int32
    )


def row_factor(tokens):
    value = tokens[...].astype(F32)
    return lax.rsqrt(jnp.mean(value * value, axis=1, keepdims=True) + 1e-06)


def attend_kernel(count, *refs):
    parts = refs[:count]
    tokens, parents, keys, values, query, result, tops, sums, scores, weights = refs[count:]
    rows, width = query.shape
    heads = width // HEAD
    cached = keys.shape[0] // rows
    total = parts[0][...].astype(F32)
    for part in parts[1:]:
        total += part[...].astype(F32)
    projected = (total * row_factor(tokens)).astype(BF)
    query[...] = projected
    span = BEAMS * cached
    groups = rows // BEAMS
    position = lax.broadcasted_iota(jnp.int32, (1, span), 1) // cached
    parent_of = column_of(parents[...])
    windows = []
    for group in range(groups):
        first = group * BEAMS
        windows.append((first // 8 * 8, -(-(first + BEAMS) // 8) * 8))
    size = max(high - low for low, high in windows)
    for group, (low, high) in enumerate(windows):
        for head in range(heads):
            at = slice(head * HEAD, (head + 1) * HEAD)
            place = (group * heads + head) * size
            scores[place : place + high - low, :] = lax.dot_general(
                projected[low:high, at],
                keys[group * span : (group + 1) * span, at],
                (((1,), (1,)), ((), ())),
                preferred_element_type=F32,
            )
    unit = HEAD ** (-0.5) * LOG2E
    marks = []
    for group, (low, high) in enumerate(windows):
        token = lax.broadcasted_iota(jnp.int32, (high - low, 1), 0) + low
        marks.append((token >= group * BEAMS) & (token < (group + 1) * BEAMS))
    lane = lax.broadcasted_iota(jnp.int32, (size, tops.shape[1]), 1)
    for group, (low, high) in enumerate(windows):
        first = group * BEAMS
        parent = jnp.where(marks[group], parent_of[low:high], -1)
        bias = jnp.where(position == parent, 0.0, LOW)
        all_tops = jnp.zeros((high - low, tops.shape[1]), F32)
        all_sums = all_tops
        for head in range(heads):
            place = (group * heads + head) * size
            score = scores[place : place + high - low, :] * unit + bias
            top = jnp.max(score, axis=1, keepdims=True)
            weight = jnp.exp2(score - top)
            mass = jnp.sum(weight, axis=1, keepdims=True)
            weights[place : place + high - low, :] = weight
            here = lane[: high - low] == head
            all_tops = jnp.where(here, top, all_tops)
            all_sums = jnp.where(here, mass, all_sums)
        for target, value in ((tops, all_tops), (sums, all_sums)):
            if low == first:
                target[low:high, :] = value
            else:
                target[low:high, :] = jnp.where(marks[group], value, target[low:high, :])
    for group, (low, high) in enumerate(windows):
        for head in range(heads):
            at = slice(head * HEAD, (head + 1) * HEAD)
            place = (group * heads + head) * size
            value = jnp.dot(
                weights[place : place + high - low, :].astype(BF),
                values[group * span : (group + 1) * span, at],
                preferred_element_type=F32,
            )
            if low == group * BEAMS:
                result[low:high, at] = value
            else:
                result[low:high, at] = jnp.where(marks[group], value, result[low:high, at])


def attend(parts, tokens, parents, keys, values):
    rows, width = parts[0].shape
    cached = keys.shape[0] // rows
    stack = rows // BEAMS * (width // HEAD) * (-(-BEAMS // 8) * 8 + 8)
    return pl.pallas_call(
        functools.partial(attend_kernel, len(parts)),
        in_specs=[VM] * (len(parts) + 4),
        out_specs=[VM] * 4,
        out_shape=[
            shape((rows, width), BF),
            shape((rows, width), F32),
            shape((rows, HEAD), F32),
            shape((rows, HEAD), F32),
        ],
        scratch_shapes=[pltpu.VMEM((stack, BEAMS * cached), F32)] * 2,
        compiler_params=params(14),
        cost_estimate=cost(4 * rows * BEAMS * cached * width, 4 * keys.size),
        name="attend",
    )(*parts, tokens, parents, keys, values)


def merge_kernel(count, *refs):
    parts = refs[:count]
    tokens, query, result, tops, sums, out = refs[count:]
    width = query.shape[1]
    total = parts[0][...].astype(F32)
    for part in parts[1:]:
        total += part[...].astype(F32)
    projected = (total * row_factor(tokens)).astype(BF).astype(F32)
    product = query[...].astype(F32) * projected[:, :width]
    unit = HEAD ** (-0.5) * LOG2E
    for head in range(width // HEAD):
        at = slice(head * HEAD, (head + 1) * HEAD)
        score = jnp.sum(product[:, at], axis=1, keepdims=True) * unit
        old = tops[:, head : head + 1]
        top = jnp.maximum(old, score)
        keep = jnp.exp2(old - top)
        weight = jnp.exp2(score - top)
        scale = 1.0 / (sums[:, head : head + 1] * keep + weight)
        value = projected[:, width + head * HEAD : width + (head + 1) * HEAD]
        out[:, at] = (result[:, at] * (keep * scale) + value * (weight * scale)).astype(BF)


def merge(parts, tokens, query, result, tops, sums):
    return pl.pallas_call(
        functools.partial(merge_kernel, len(parts)),
        in_specs=[VM] * (len(parts) + 5),
        out_specs=VM,
        out_shape=shape(query.shape, BF),
        compiler_params=params(8),
        cost_estimate=cost(query.size * 8, query.size * 8),
        name="merge",
    )(*parts, tokens, query, result, tops, sums)


def output_kernel(chips, place, *refs):
    pieces, (own_w, other_w), outs = refs[:chips], refs[chips : chips + 2], refs[chips + 2 :]
    rows = pieces[0].shape[0]
    half = own_w.shape[1]
    joined = jnp.concatenate([piece[...].astype(F32) for piece in pieces], axis=0).astype(BF)
    for at, weight in ((place[0], own_w), (1 - place[0], other_w)):
        columns = pl.ds(pl.multiple_of(at * half, half), half)
        total = jnp.dot(joined, weight[...], preferred_element_type=F32)
        for k in range(chips):
            outs[k][:, columns] = total[k * rows : (k + 1) * rows].astype(BF)


def output(place, pieces, own_w, other_w):
    chips = len(pieces)
    rows = pieces[0].shape[0]
    width, half = own_w.shape
    return pl.pallas_call(
        functools.partial(output_kernel, chips),
        in_specs=[SM] + [VM] * (chips + 2),
        out_specs=[VM] * chips,
        out_shape=[shape((rows, CORES * half), BF)] * chips,
        compiler_params=params(16),
        cost_estimate=cost(4 * chips * rows * width * half, 4 * width * half),
        name="output",
    )(place, *pieces, own_w, other_w)


def logits_kernel(count, place, *refs):
    partials, (tokens, gain, weight, allowed) = refs[:count], refs[count : count + 4]
    own_stream, own_tail, outs = refs[count + 4], refs[count + 5], refs[count + 6 :]
    rows, width = tokens.shape
    value = partials[0][...].astype(F32)
    for partial in partials[1:]:
        value += partial[...].astype(F32)
    value += tokens[...].astype(F32)
    rounded = value.astype(BF)
    own_stream[...] = rounded
    for out in outs:
        out[:, :width] = rounded
    square = jnp.sum(value * value, axis=1, keepdims=True)
    scaled = gain[:, pl.ds(pl.multiple_of(place[1] * width, width), width)]
    whole = jnp.dot((value * scaled).astype(BF), weight[...], preferred_element_type=F32)
    picked = []
    for slot in range(allowed.shape[0]):
        wanted = column_of(allowed[slot : slot + 1, :])
        total = jnp.zeros((rows, BLOCK), F32)
        for block in range(whole.shape[1] // BLOCK):
            total = jnp.where(
                wanted == block, whole[:, block * BLOCK : (block + 1) * BLOCK], total
            )
        picked.append(total)
    picked = jnp.concatenate(picked, axis=1)
    share = picked.shape[1] // count
    wide = own_tail.shape[1]
    lane = lax.broadcasted_iota(jnp.int32, (rows, wide), 1)
    coarse = square.astype(BF).astype(F32)
    tail = jnp.where(lane == share, coarse, jnp.where(lane == share + 1, square - coarse, 0.0))
    blocks = []
    for target in range(count):
        cut = picked[:, target * share : (target + 1) * share]
        blocks.append(jnp.concatenate([cut, tail[:, share:]], axis=1))
    for shift in range(count):
        target = lax.rem(place[1] + shift, count)
        total = blocks[0]
        for index in range(1, count):
            total = jnp.where(target == index, blocks[index], total)
        if shift == 0:
            own_tail[...] = total
        else:
            outs[shift - 1][:, width:] = total.astype(BF)


def logits(place, partials, tokens, gain, weight, allowed):
    count = len(partials)
    rows, width = tokens.shape
    share = allowed.shape[0] * BLOCK // count
    wide = (share + 1 + BLOCK) // BLOCK * BLOCK
    return pl.pallas_call(
        functools.partial(logits_kernel, count),
        in_specs=[SM] + [VM] * (count + 4),
        out_specs=[VM] * (count + 1),
        out_shape=[shape((rows, width), BF), shape((rows, wide), F32)]
        + [shape((rows, width + wide), BF)] * (count - 1),
        compiler_params=params(8),
        cost_estimate=cost(2 * rows * weight.shape[0] * weight.shape[1], 2 * weight.size),
        name="logits",
    )(place, *partials, tokens, gain, weight, allowed)


def finish_kernel(count, share, place, own_stream, own_tail, *refs):
    others, (stream_out, logits_out) = refs[: count - 1], refs[-2:]
    width = own_stream.shape[1]

    def columns(shift):
        owner = lax.rem(place[1] + count - shift, count)
        return pl.ds(pl.multiple_of(owner * width, width), width)

    stream_out[:, columns(0)] = own_stream[...]
    total = own_tail[...]
    for shift in range(1, count):
        stream_out[:, columns(shift)] = others[shift - 1][:, :width]
        total += others[shift - 1][:, width:].astype(F32)
    square = total[:, share : share + 1] + total[:, share + 1 : share + 2]
    factor = lax.rsqrt(square * (1.0 / (count * width)) + 1e-06)
    logits_out[...] = total[:, :share] * factor


def finish(place, own_stream, own_tail, others, share):
    count = len(others) + 1
    rows, width = own_stream.shape
    return pl.pallas_call(
        functools.partial(finish_kernel, count, share),
        in_specs=[SM] + [VM] * (count + 1),
        out_specs=[VM, VM],
        out_shape=[shape((rows, count * width), BF), shape((rows, share), F32)],
        compiler_params=params(4),
        name="finish",
    )(place, own_stream, own_tail, *others)


def on_device(
    dp,
    mp,
    tokens,
    attn_gain,
    head_gain,
    qkv_weight,
    out_weight,
    head_weight,
    key_cache,
    value_cache,
    parents,
    allowed,
):
    chips = dp // CORES
    rows = tokens.shape[0]
    here = lax.axis_index("dp")
    level = lax.axis_index("mp")
    chip, core = here // CORES, here % CORES
    place = jnp.stack([core, level, chip]).astype(jnp.int32)

    def to_chip(value, k):
        return lax.ppermute(value, "dp", [(i, i ^ (CORES * k)) for i in range(dp)])

    def to_level(value, m):
        return lax.ppermute(value, "mp", [(i, (i + m) % mp) for i in range(mp)])

    def to_core(value):
        return lax.ppermute(value, "dp", [(i, i ^ 1) for i in range(dp)])

    def spread(values):
        return list(values[:1]) + [to_chip(values[k], k) for k in range(1, chips)]

    def after(value, *earlier):
        return lax.optimization_barrier((value, *earlier))[0]

    *blocks, level_tokens = split(place, tokens, chips)
    all_qkv = jnp.transpose(qkv_weight, (1, 0, 2)).reshape(-1, qkv_weight.shape[2])
    other_qkv = to_core(all_qkv)
    other_out = to_core(out_weight)
    pieces = spread(blocks)
    head_width = key_cache.shape[2]
    caches = (key_cache.reshape(-1, head_width), value_cache.reshape(-1, head_width))
    own_qkv, keys, values = fetch("fetch", *after((all_qkv, *caches), blocks[0]))

    *parts, own_x, other_x = project_query(
        place, pieces, attn_gain[None], own_qkv, other_qkv
    )
    parts = spread(parts)
    pairs = spread(project_pair(own_x, other_x, own_qkv, other_qkv, chips))
    seen = attend(parts, tokens, parents[None], keys, values)
    attended = merge(pairs, tokens, *seen)

    pieces = spread([attended] * chips)
    own_out, other_out = fetch("fetch_out", *after((out_weight, other_out), attended))
    parts = list(output(place, pieces, own_out, other_out))
    parts = jnp.stack(parts[:1] + [to_chip(parts[k], k) for k in range(1, chips)])
    slices = [
        lax.dynamic_index_in_dim(parts, chip ^ ((level + m) % mp), 0, keepdims=False)
        for m in range(mp)
    ]
    slices = slices[:1] + [to_level(slices[m], m) for m in range(1, mp)]
    own_stream, own_tail, *others = logits(
        place, slices, level_tokens, head_gain[None], head_weight, allowed.T
    )
    others = [to_level(other, m + 1) for m, other in enumerate(others)]
    return tuple(finish(place, own_stream, own_tail, others, allowed.shape[1] * BLOCK // mp))


def solution(mesh):
    in_specs = (
        P("dp", None),
        P(),
        P(),
        P("dp", None, "mp"),
        P("mp", "dp"),
        P("mp", None),
        P("dp", None, "mp"),
        P("dp", None, "mp"),
        P("dp"),
        P("dp", None),
    )
    out_specs = (P("dp", None), P("dp", "mp"))
    return jax.shard_map(
        functools.partial(on_device, mesh.shape["dp"], mesh.shape["mp"]),
        mesh=mesh,
        in_specs=in_specs,
        out_specs=out_specs,
        check_vma=False,
    )
```
